512 devices in a mesh: dp: 8 (over y, core), expert: 64 (over z, x).
Axes of the slice: x: 4, y: 4, z: 16, core: 2. Of those that a mesh axis runs over, the one named last changes fastest.
Arguments:
- tokens: bfloat16 [98304, 2048], P(('dp', 'expert')), may hold values from -6 to 6
- routing: int32 [98304, 1], P(('dp', 'expert')), may hold values from 0 to 63; in each aligned block of 192 rows (0 to 191, 192 to 383, ...) at most 6 rows name the same one
- gate_scale: float32 [98304, 1], P(('dp', 'expert')), may hold values from 0.25 to 1
- cotangent: bfloat16 [98304, 2048], P(('dp', 'expert')), may hold values from -6 to 6
- up_weight: bfloat16 [64, 512, 2048], P('expert', 'dp'), may hold values from -0.125 to 0.125
- down_weight: bfloat16 [64, 512, 2048], P('expert', 'dp'), may hold values from -0.25 to 0.25
Outputs:
- output_rows: bfloat16 [98304, 2048], P(('dp', 'expert'))
- token_grad: bfloat16 [98304, 2048], P(('dp', 'expert'))
- grad_up: bfloat16 [64, 512, 2048], P('expert', 'dp')
- grad_down: bfloat16 [64, 512, 2048], P('expert', 'dp')
The draws below stay inside these ranges and needn't reach their ends.
Inputs may be any that keep to these rules, and one draw needn't show every extreme that they name: `routing`: within the 192 tokens of one device, each expert is named by at most 6 tokens, a bound that some block reaches.
All inputs are finite; a program needn't handle non-finite values.
Results may differ from the reference program's by a relative error of at most 0.014.
Values may be sent and summed in bfloat16 or wider, within the bound.
No kernel may reach another device: no remote copies, remote signals or barrier semaphores. Data moves between devices by JAX's collectives and lax.ppermute only.
A program may use at most 64 MiB of HBM per device.

```python
import math
import jax
import jax.numpy as jnp
import numpy as np
from jax import lax

D = 2048
FF = 512
TOK_DEV = 192
EXPERTS = 64
CAP = 6
TOKENS = 98304
N_DP = 8
N_EXPERT = 64


def level_of(rng, dims, shards, low, largest):
    def one(position, parts):
        steps = jax.random.uniform(jax.random.fold_in(jax.random.fold_in(rng, 6), position), (parts,), jnp.float32, low / len(shards), largest / len(shards))
        return jnp.repeat(jnp.exp(steps), dims[position] // parts).reshape((-1,) + (1,) * (len(dims) - position - 1))

    gain = one(*shards[0])
    for cut in shards[1:]:
        gain = gain * one(*cut)
    return gain


def deal_out(own_key, own, number, rows, count, top, reach, skew):
    order = jax.random.permutation(own_key, count)
    crowded, common = load_shares(count, rows * top, reach, skew, True), load_shares(count, rows * top, reach, skew, False)
    places = jnp.arange(count)

    def named(tallies, offset_by):
        used = int((tallies > 0).sum())
        fixed = max(1, used // 4)
        moved = fixed + (places - fixed + offset_by * (used - fixed)) % max(1, count - fixed)
        return jnp.zeros((count,), jnp.int32).at[order[jnp.where(places < fixed, places, moved)]].set(jnp.asarray(tallies, jnp.int32))

    tallies = jnp.where(number % 4 == 0, named(crowded, number // 4), named(common, number - number // 4 - 1))
    mixed = jax.random.permutation(jax.random.fold_in(own, 3), count)
    giver, taker = mixed[0:count // 2 * 2:2], mixed[1:count // 2 * 2:2]
    slack = jnp.minimum(tallies[giver] - 1, reach - tallies[taker]) // 2
    slack = jnp.where((giver == order[0]) | (taker == order[0]) | (tallies[taker] == 0), 0, jnp.maximum(slack, 0))
    moved = jax.random.randint(jax.random.fold_in(own, 4), (count // 2,), 0, 1 << 20) % (slack + 1)
    tallies = tallies.at[giver].add(-moved).at[taker].add(moved)
    items = jnp.searchsorted(jnp.cumsum(tallies), jnp.arange(rows * top), side="right").astype(jnp.int32)
    listing = items.reshape(top, rows).T
    listing = listing[jax.random.permutation(jax.random.fold_in(own, 1), rows)]
    offset_by = jax.random.randint(jax.random.fold_in(own, 2), (rows, 1), 0, top)
    return jnp.take_along_axis(listing, (jnp.arange(top)[None, :] + offset_by) % top, axis=1)


def load_shares(count, total, reach, slope, full):
    portions = [(1 << 20) // math.isqrt(grade ** slope) + 1 for grade in range(1, count + 1)]
    largest = reach if full else min(reach, max(-(-total // count), total * portions[0] // sum(portions)))
    least = 1 if total - largest >= count - 1 else 0
    counts, spare = [largest] + [least] * (count - 1), total - largest - least * (count - 1)
    while spare > 0:
        free = [i for i in range(1, count) if counts[i] < largest] or [i for i in range(1, count) if counts[i] < reach]
        pool, remaining = sum([portions[i] for i in free]), spare
        for i in free:
            more = min(reach - counts[i], max(1, remaining * portions[i] // pool), spare)
            counts[i] = counts[i] + more
            spare = spare - more
    return np.array(counts)


def gaussian(own_key, dims, spread, bound, cuts=(), kind=jnp.bfloat16):
    loudness = level_of(own_key, dims, cuts, -0.22, 0.18) if cuts else 1.0
    values = jax.random.normal(own_key, dims, jnp.float32) * spread * loudness
    return jnp.minimum(jnp.maximum(values, -bound), bound).astype(kind)


def setup_inputs(seed: int = 0) -> dict:
    splits = jax.random.split(jax.random.key(seed), 7)
    tokens = gaussian(splits[0], (TOKENS, D), 1.0, 6.0, ((0, 512),))
    routing_keys = jax.random.split(jax.random.fold_in(splits[1], 1), TOKENS // TOK_DEV)
    routing_turns = jax.random.permutation(jax.random.fold_in(splits[1], 3), TOKENS // TOK_DEV)
    routing = jax.vmap(lambda own, number: deal_out(jax.random.fold_in(splits[1], 2), own, number, TOK_DEV, EXPERTS, 1, CAP, 2))(routing_keys, routing_turns).reshape((TOKENS, 1))
    gate_scale = jnp.clip(jnp.exp(math.log(1.0) - 1.3862944 * jax.random.uniform(splits[2], (TOKENS, 1), jnp.float32) ** level_of(splits[2], (TOKENS, 1), ((0, 512),), -0.2, 0.2)), 0.25, 1.0)
    cotangent = gaussian(splits[3], (TOKENS, D), 1.0, 6.0, ((0, 512),))
    up_weight = gaussian(splits[4], (EXPERTS, FF, D), D ** -0.5, 0.125, ((0, 64), (1, 8)))
    down_weight = gaussian(splits[5], (EXPERTS, FF, D), FF ** -0.5, 0.25, ((0, 64), (1, 8)))
    return {"tokens": tokens, "routing": routing, "gate_scale": gate_scale, "cotangent": cotangent, "up_weight": up_weight, "down_weight": down_weight}


def smooth(values):
    return jax.nn.gelu(values, approximate=True)

def reference(tokens, routing, gate_scale, cotangent, up_weight, down_weight):
    devices = N_DP * N_EXPERT
    ids = routing.reshape(devices, TOK_DEV).astype(jnp.int32)
    onehot = (ids[:, :, None] == jnp.arange(EXPERTS, dtype=jnp.int32)[None, None, :]).astype(jnp.int32)
    slot_rank = lax.optimization_barrier(jnp.sum(jnp.cumsum(onehot, axis=1) * onehot, axis=2)).astype(jnp.int32) - 1
    source = (jnp.arange(devices, dtype=jnp.int32) % N_EXPERT).astype(jnp.int32)
    slot_row = (source[:, None] * CAP + slot_rank).astype(jnp.int32).reshape(N_DP, N_EXPERT * TOK_DEV)
    group_ids = ids.reshape(N_DP, N_EXPERT * TOK_DEV)
    group_tokens = tokens.reshape(N_DP, N_EXPERT * TOK_DEV, D)
    scaled = (gate_scale * cotangent.astype(jnp.float32)).astype(jnp.bfloat16)
    group_scaled = scaled.reshape(N_DP, N_EXPERT * TOK_DEV, D)
    up_full = up_weight.astype(jnp.float32)
    down_full = down_weight.astype(jnp.float32)

    def group(carry, inputs):
        expert_ids, rows, inputs_tok, inputs_cot = inputs
        empty = jnp.zeros((EXPERTS, N_EXPERT * CAP, D), jnp.bfloat16)
        buffer = empty.at[expert_ids, rows].set(inputs_tok)
        dbuffer = empty.at[expert_ids, rows].set(inputs_cot)
        buffer_f = buffer.astype(jnp.float32)
        dbuffer_f = dbuffer.astype(jnp.float32)
        preact = jnp.einsum('erd,efd->erf', buffer_f, up_full)
        hidden = smooth(preact).astype(jnp.bfloat16)
        expert_out = jnp.einsum('erf,efd->erd', hidden.astype(jnp.float32), down_full).astype(jnp.bfloat16)
        hidden_grad = jnp.einsum('erd,efd->erf', dbuffer_f, down_full)
        unused, backward = jax.vjp(smooth, preact)
        preact_grad = backward(hidden_grad)[0].astype(jnp.bfloat16)
        slot_grad = jnp.einsum('erf,efd->erd', preact_grad.astype(jnp.float32), up_full).astype(jnp.bfloat16)
        term_up = jnp.einsum('erf,erd->efd', preact_grad.astype(jnp.float32), buffer_f).astype(jnp.bfloat16)
        term_down = jnp.einsum('erf,erd->efd', hidden.astype(jnp.float32), dbuffer_f).astype(jnp.bfloat16)
        new_carry = (carry[0] + term_up.astype(jnp.float32), carry[1] + term_down.astype(jnp.float32))
        return (new_carry, (expert_out[expert_ids, rows], slot_grad[expert_ids, rows]))
    start = (jnp.zeros((EXPERTS, FF, D), jnp.float32), jnp.zeros((EXPERTS, FF, D), jnp.float32))
    sums, picked = lax.scan(group, start, (group_ids, slot_row, group_tokens, group_scaled))
    out_pick = picked[0].reshape(TOKENS, D)
    grad_pick = picked[1].reshape(TOKENS, D)
    output_rows = (gate_scale * out_pick.astype(jnp.float32)).astype(jnp.bfloat16)
    return (output_rows, grad_pick, sums[0].astype(jnp.bfloat16), sums[1].astype(jnp.bfloat16))
```

```python
import jax
import jax.numpy as jnp
from jax import lax
from jax.sharding import Mesh
from jax.sharding import PartitionSpec as P

DP = ("y", "core")
SLAB = ("y", "core", "x")
EVERY = ("y", "core", "z", "x")
ROWS = 8


def smooth(values):
    return jax.nn.gelu(values, approximate=True)


def exchange(values, axes):
    return lax.all_to_all(values, axes, split_axis=0, concat_axis=0, tiled=True)


def cols(left, right):
    return lax.dot_general(
        left, right, (((1,), (1,)), ((), ())), preferred_element_type=jnp.float32
    )


def rows(left, right):
    return lax.dot_general(
        left, right, (((0,), (0,)), ((), ())), preferred_element_type=jnp.float32
    )


def plain(left, right):
    return jnp.dot(left, right, preferred_element_type=jnp.float32)


def per_device(tokens, routing, gate_scale, cotangent, up_weight, down_weight):
    count, width = tokens.shape
    n_z, n_x = lax.axis_size("z"), lax.axis_size("x")
    n_dp = lax.axis_size("y") * lax.axis_size("core")
    held = n_z // n_dp
    units = up_weight.shape[1]
    block = width // n_z
    places = n_dp * n_x
    slot_total = places * held * ROWS
    taken = places * ROWS

    up_all = lax.all_gather(up_weight[0], "z", axis=0, tiled=False)
    up_own = exchange(up_all.reshape(n_dp, held * units, width), DP)
    up_own = up_own.reshape(n_dp, held, units, width)
    down_cut = down_weight[0].reshape(units, n_z, block).transpose(1, 0, 2)
    down_cut = exchange(down_cut, "z").reshape(n_dp, held * units, block)
    down_cut = exchange(down_cut, DP)
    down_own = lax.all_gather(down_cut, "z", axis=0, tiled=False)
    down_own = down_own.reshape(n_z, n_dp, held, units, block)
    up = [up_own[:, k].reshape(n_dp * units, width) for k in range(held)]
    down = [
        down_own[:, :, k].transpose(1, 2, 0, 3).reshape(n_dp * units, width)
        for k in range(held)
    ]

    ids = routing[:, 0]
    onehot = (ids[:, None] == jnp.arange(n_z * n_x, dtype=jnp.int32)[None, :]).astype(jnp.float32)
    position = jnp.arange(count, dtype=jnp.int32)
    lower_tri = (position[:, None] >= position[None, :]).astype(jnp.float32)
    counts = plain(lower_tri, onehot)
    slot_rank = (jnp.sum(counts * onehot, axis=1) - 1.0).astype(jnp.int32)
    at_z, at_x = ids // n_x, ids % n_x
    slot_index = (((at_z // held) * n_x + at_x) * held + at_z % held) * ROWS + slot_rank
    placer = (jnp.arange(slot_total, dtype=jnp.int32)[:, None] == slot_index[None, :]).astype(
        jnp.bfloat16
    )

    def place(values):
        placed = plain(placer, values).astype(jnp.bfloat16)
        return placed.reshape(places, held * ROWS, width)

    scaled = (gate_scale * cotangent.astype(jnp.float32)).astype(jnp.bfloat16)
    tok = exchange(place(tokens), SLAB).reshape(places, held, ROWS, width)
    cot = exchange(place(scaled), SLAB).reshape(places, held, ROWS, width)
    tok = [tok[:, k].reshape(taken, width) for k in range(held)]
    cot = [cot[:, k].reshape(taken, width) for k in range(held)]

    preact = [cols(tok[k], up[k]) for k in range(held)]
    hidden = [smooth(preact[k]).astype(jnp.bfloat16) for k in range(held)]
    term_down = jnp.stack([rows(hidden[k], cot[k]).astype(jnp.bfloat16) for k in range(held)])

    sum_down = term_down.reshape(held, n_dp * units, n_z, block).transpose(2, 0, 1, 3)
    sum_down = lax.psum_scatter(sum_down, "z", scatter_dimension=0, tiled=True)
    sum_down = sum_down.reshape(held, n_dp, units, block).transpose(1, 0, 2, 3)
    sum_down = exchange(sum_down.reshape(n_dp, held * units, block), DP)
    sum_down = exchange(sum_down.reshape(n_z, units, block), "z")
    grad_down = sum_down.transpose(1, 0, 2).reshape(1, units, width)

    hidden_grad = [cols(cot[k], down[k]) for k in range(held)]
    preact_grad = [
        jax.vjp(smooth, preact[k])[1](hidden_grad[k])[0].astype(jnp.bfloat16) for k in range(held)
    ]
    term_up = jnp.stack(
        [
            rows(preact_grad[k], tok[k]).astype(jnp.bfloat16).reshape(n_dp, units, width)
            for k in range(held)
        ],
        axis=1,
    )
    sum_up = exchange(term_up.reshape(n_dp, held * units, width), DP)
    sum_up = lax.psum_scatter(
        sum_up.reshape(n_z, units, width), "z", scatter_dimension=0, tiled=True
    )
    grad_up = sum_up.reshape(1, units, width)

    def back(values):
        values = [v.astype(jnp.bfloat16).reshape(places, ROWS, width) for v in values]
        values = jnp.stack(values, axis=1).reshape(places, held * ROWS, width)
        return rows(placer, exchange(values, SLAB).reshape(slot_total, width))

    output = back([plain(hidden[k], down[k]) for k in range(held)])
    output_rows = (gate_scale * output).astype(jnp.bfloat16)
    token_grad = back([plain(preact_grad[k], up[k]) for k in range(held)]).astype(jnp.bfloat16)
    return (output_rows, token_grad, grad_up, grad_down)


def solution(mesh):
    finer = Mesh(mesh.devices.reshape(4, 2, 16, 4), EVERY)
    spread = P(EVERY, None)
    stored = P(("z", "x"), DP, None)
    specs = (spread, spread, stored, stored)
    return jax.shard_map(
        per_device,
        mesh=finer,
        in_specs=(spread, spread, spread, spread, stored, stored),
        out_specs=specs,
        check_vma=False,
    )
```

```python
import jax
import jax.numpy as jnp
from jax import lax
from jax.sharding import Mesh
from jax.sharding import PartitionSpec as P


DP = ("y", "core")
BLOCK = ("y", "core", "near", "x")
EVERY = ("y", "core", "far", "near", "x")
EXPERT = ("far", "near", "x")
ROWS = 8


def smooth(values):
    return jax.nn.gelu(values, approximate=True)


def exchange(values, axes):
    return lax.all_to_all(values, axes, split_axis=0, concat_axis=0, tiled=True)


def cols(left, right):
    return lax.dot_general(
        left, right, (((1,), (1,)), ((), ())), preferred_element_type=jnp.float32
    )


def rows(left, right):
    return lax.dot_general(
        left, right, (((0,), (0,)), ((), ())), preferred_element_type=jnp.float32
    )


def plain(left, right):
    return jnp.dot(left, right, preferred_element_type=jnp.float32)


def step(tokens, routing, gate_scale, cotangent, up_weight, down_weight):
    count, width = tokens.shape
    n_far = lax.axis_size("far")
    units = up_weight.shape[1]
    experts = lax.axis_size(BLOCK)
    taken = experts * ROWS

    def gather(shard):
        return lax.all_gather(shard[0], "far", axis=0, tiled=False)

    def by_owner(term):
        return exchange(term.astype(jnp.bfloat16).reshape(n_far, units, width), DP)

    def summed(parts):
        return lax.psum_scatter(parts, "far", scatter_dimension=0, tiled=True)

    def whole(parts):
        return exchange(parts, DP).reshape(n_far * units, width)

    ids = routing[:, 0]
    onehot = (ids[:, None] == jnp.arange(experts, dtype=jnp.int32)[None, :]).astype(jnp.float32)
    position = jnp.arange(count, dtype=jnp.int32)
    lower_tri = (position[:, None] >= position[None, :]).astype(jnp.float32)
    counts = plain(lower_tri, onehot)
    slot_rank = (jnp.sum(counts * onehot, axis=1) - 1.0).astype(jnp.int32)
    slot_index = ids * ROWS + slot_rank
    placer = (jnp.arange(taken, dtype=jnp.int32)[:, None] == slot_index[None, :]).astype(
        jnp.bfloat16
    )

    def across(left, right):
        both = jnp.concatenate((left, right), axis=1).astype(jnp.bfloat16)
        both = exchange(both.reshape(experts, ROWS, 2 * width), BLOCK)
        return both.reshape(taken, 2 * width)

    scaled = (gate_scale * cotangent.astype(jnp.float32)).astype(jnp.bfloat16)
    up_parts = gather(up_weight)
    down_parts = gather(down_weight)
    arrived = across(plain(placer, tokens), plain(placer, scaled))
    arrived, up_parts = lax.optimization_barrier((arrived, up_parts))
    tok, cot = arrived[:, :width], arrived[:, width:]
    up = whole(up_parts)
    preact = cols(tok, up)
    hidden = smooth(preact).astype(jnp.bfloat16)
    down_term = by_owner(rows(hidden, cot))
    down_term, down_parts = lax.optimization_barrier((down_term, down_parts))
    grad_down = summed(down_term)
    down = whole(down_parts)
    hidden_grad = cols(cot, down)
    preact_grad = jax.vjp(smooth, preact)[1](hidden_grad)[0].astype(jnp.bfloat16)
    up_term = by_owner(rows(preact_grad, tok))
    up_term, hidden, preact_grad = lax.optimization_barrier((up_term, hidden, preact_grad))
    grad_up = summed(up_term)
    returned = across(plain(hidden, down), plain(preact_grad, up))
    output_rows = (gate_scale * rows(placer, returned[:, :width])).astype(jnp.bfloat16)
    token_grad = rows(placer, returned[:, width:]).astype(jnp.bfloat16)
    return (output_rows, token_grad, grad_up, grad_down)


def solution(mesh):
    finer = Mesh(mesh.devices.reshape(4, 2, 8, 2, 4), EVERY)
    spread = P(EVERY, None)
    stored = P(EXPERT, DP, None)
    specs = (spread, spread, stored, stored)
    return jax.shard_map(
        step,
        mesh=finer,
        in_specs=(spread, spread, spread, spread, stored, stored),
        out_specs=specs,
        check_vma=False,
    )
```

```python
import jax
import jax.numpy as jnp
from jax import lax
from jax.sharding import Mesh
from jax.sharding import PartitionSpec as P


EVERY = ("y", "core", "far", "near", "x")
EXPERT = ("far", "near", "x")
ROWS = 6


def smooth(values):
    return jax.nn.gelu(values, approximate=True)


def exchange(values, axes):
    return lax.all_to_all(values, axes, split_axis=0, concat_axis=0, tiled=True)


def cols(left, right):
    return lax.dot_general(
        left, right, (((1,), (1,)), ((), ())), preferred_element_type=jnp.float32
    )


def rows(left, right):
    return lax.dot_general(
        left, right, (((0,), (0,)), ((), ())), preferred_element_type=jnp.float32
    )


def plain(left, right):
    return jnp.dot(left, right, preferred_element_type=jnp.float32)


def swap_core(values):
    return lax.ppermute(values, "core", [(0, 1), (1, 0)])


def shift(values, step, z_total):
    pairs = []
    for core in range(2):
        move = -step if core == 1 and step in (2, -2) else step
        for z in range(z_total):
            pairs.append((core * z_total + z, core * z_total + (z + move) % z_total))
    return lax.ppermute(values, ("core", "far", "near"), pairs)


def step(tokens, routing, gate_scale, cotangent, up_weight, down_weight):
    count, width = tokens.shape
    units = up_weight.shape[1]
    n_far, n_near, n_x = lax.axis_size("far"), lax.axis_size("near"), lax.axis_size("x")
    z_total = n_far * n_near
    places = n_far * n_x
    part = places * ROWS
    taken = n_near * part
    steps = (0, 1, 2, -1)

    def gather(shard):
        return lax.all_gather(shard[0], "far", axis=0, tiled=False)

    def whole(parts):
        own = exchange(parts, "y")
        return own.reshape(n_far * units, width)

    def by_owner(own, other):
        own = (own + swap_core(other.astype(jnp.bfloat16)).astype(jnp.float32))
        own = own.astype(jnp.bfloat16).reshape(n_far, units, width)
        return exchange(own, "y")

    def summed(parts):
        return lax.psum_scatter(parts, "far", scatter_dimension=0, tiled=True)

    ids = routing[:, 0]
    experts = z_total * n_x
    onehot = (ids[:, None] == jnp.arange(experts, dtype=jnp.int32)[None, :]).astype(jnp.float32)
    position = jnp.arange(count, dtype=jnp.int32)
    lower_tri = (position[:, None] >= position[None, :]).astype(jnp.float32)
    counts = plain(lower_tri, onehot)
    slot_rank = (jnp.sum(counts * onehot, axis=1) - 1.0).astype(jnp.int32)
    at_z, at_x = ids // n_x, ids % n_x
    away = (at_z % n_near - lax.axis_index("near") + n_near) % n_near
    slot_index = away * part + ((at_z // n_near) * n_x + at_x) * ROWS + slot_rank
    placer = (jnp.arange(taken, dtype=jnp.int32)[:, None] == slot_index[None, :]).astype(
        jnp.bfloat16
    )
    row = jnp.arange(taken, dtype=jnp.int32)
    source = (row // ROWS) % n_near * part + row // (n_near * ROWS) * ROWS + row % ROWS
    order = (source[:, None] == row[None, :]).astype(jnp.bfloat16)

    scaled = (gate_scale * cotangent.astype(jnp.float32)).astype(jnp.bfloat16)
    up_parts = gather(up_weight)
    down_parts = gather(down_weight)
    both = jnp.concatenate((tokens, scaled), axis=1)
    pieces = []
    for k in range(n_near):
        piece = plain(placer[k * part : (k + 1) * part], both).astype(jnp.bfloat16)
        if steps[k]:
            piece = shift(piece, steps[k], z_total)
        pieces.append(piece)
    arrived = plain(order, jnp.concatenate(pieces, axis=0)).astype(jnp.bfloat16)
    arrived = exchange(arrived.reshape(places, n_near * ROWS, 2 * width), ("y", "x"))
    arrived = arrived.reshape(taken, 2 * width)
    arrived, up_parts = lax.optimization_barrier((arrived, up_parts))
    tok, cot = arrived[:, :width], arrived[:, width:]

    up = whole(up_parts)
    up = (up, swap_core(up))
    down_parts, up = lax.optimization_barrier((down_parts, up))
    down = whole(down_parts)
    down = (down, swap_core(down))

    preact = [cols(tok, w) for w in up]
    hidden = [smooth(v).astype(jnp.bfloat16) for v in preact]
    down_term = by_owner(*[rows(h, cot) for h in hidden])
    grad_down = summed(down_term)

    hidden_grad = [cols(cot, w) for w in down]
    preact_grad = [
        jax.vjp(smooth, v)[1](g)[0].astype(jnp.bfloat16) for v, g in zip(preact, hidden_grad)
    ]
    up_term = by_owner(*[rows(g, tok) for g in preact_grad])
    grad_up = summed(up_term)

    out = plain(hidden[0], down[0]) + plain(hidden[1], down[1])
    slot_grad = plain(preact_grad[0], up[0]) + plain(preact_grad[1], up[1])
    back = jnp.concatenate((out, slot_grad), axis=1).astype(jnp.bfloat16)
    back = exchange(back.reshape(places, n_near * ROWS, 2 * width), ("y", "x"))
    back = rows(order, back.reshape(taken, 2 * width)).astype(jnp.bfloat16)
    pieces = []
    for k in range(n_near):
        piece = back[k * part : (k + 1) * part]
        if steps[k]:
            piece = shift(piece, -steps[k], z_total)
        pieces.append(piece)
    returned = jnp.concatenate(pieces, axis=0)
    output_rows = (gate_scale * rows(placer, returned[:, :width])).astype(jnp.bfloat16)
    token_grad = rows(placer, returned[:, width:]).astype(jnp.bfloat16)
    return (output_rows, token_grad, grad_up, grad_down)


def build(finer):
    spread = P(EVERY, None)
    stored = P(EXPERT, ("y", "core"), None)
    specs = (spread, spread, stored, stored)
    return jax.shard_map(
        step,
        mesh=finer,
        in_specs=(spread, spread, spread, spread, stored, stored),
        out_specs=specs,
        check_vma=False,
    )


def solution(mesh):
    return build(Mesh(mesh.devices.reshape(4, 2, 4, 4, 4), EVERY))
```

```python
import jax
import jax.numpy as jnp
from jax import lax
from jax.sharding import Mesh
from jax.sharding import PartitionSpec as P


EVERY = ("y", "core", "far", "near", "x")
EXPERT = ("far", "near", "x")
ROWS = 6
FAR_STEPS = (1, -1, 2)


def smooth(values):
    return jax.nn.gelu(values, approximate=True)


def exchange(values, axes):
    return lax.all_to_all(values, axes, split_axis=0, concat_axis=0, tiled=True)


def cols(left, right):
    return lax.dot_general(
        left, right, (((1,), (1,)), ((), ())), preferred_element_type=jnp.float32
    )


def rows(left, right):
    return lax.dot_general(
        left, right, (((0,), (0,)), ((), ())), preferred_element_type=jnp.float32
    )


def plain(left, right):
    return jnp.dot(left, right, preferred_element_type=jnp.float32)


def swap_core(values):
    return lax.ppermute(values, "core", [(0, 1), (1, 0)])


def shift(values, step, z_total):
    pairs = []
    for core in range(2):
        move = -step if core == 1 and step in (2, -2, z_total // 2) else step
        for z in range(z_total):
            pairs.append((core * z_total + z, core * z_total + (z + move) % z_total))
    return lax.ppermute(values, ("core", "far", "near"), pairs)


def step(tokens, routing, gate_scale, cotangent, up_weight, down_weight):
    count, width = tokens.shape
    units = up_weight.shape[1]
    n_far, n_near, n_x = lax.axis_size("far"), lax.axis_size("near"), lax.axis_size("x")
    z_total = n_far * n_near
    places = n_far * n_x
    part = places * ROWS
    taken = n_near * part
    steps = (0, 1, 2, -1)

    def gather(shard):
        return lax.all_gather(shard[0], "far", axis=0, tiled=False)

    def whole(parts):
        own = exchange(parts, "y")
        return own.reshape(n_far * units, width)

    def by_owner(own, other):
        own = (own + swap_core(other.astype(jnp.bfloat16)).astype(jnp.float32))
        own = own.astype(jnp.bfloat16).reshape(n_far, units, width)
        return exchange(own, "y")

    def summed(parts):
        return lax.psum_scatter(parts, "far", scatter_dimension=0, tiled=True)

    ids = routing[:, 0]
    experts = z_total * n_x
    onehot = (ids[:, None] == jnp.arange(experts, dtype=jnp.int32)[None, :]).astype(jnp.float32)
    position = jnp.arange(count, dtype=jnp.int32)
    lower_tri = (position[:, None] >= position[None, :]).astype(jnp.float32)
    counts = plain(lower_tri, onehot)
    slot_rank = (jnp.sum(counts * onehot, axis=1) - 1.0).astype(jnp.int32)
    at_z, at_x = ids // n_x, ids % n_x
    away = (at_z % n_near - lax.axis_index("near") + n_near) % n_near
    slot_index = away * part + ((at_z // n_near) * n_x + at_x) * ROWS + slot_rank
    placer = (jnp.arange(taken, dtype=jnp.int32)[:, None] == slot_index[None, :]).astype(
        jnp.bfloat16
    )
    row = jnp.arange(taken, dtype=jnp.int32)
    source = (row // ROWS) % n_near * part + row // (n_near * ROWS) * ROWS + row % ROWS
    order = (source[:, None] == row[None, :]).astype(jnp.bfloat16)

    scaled = (gate_scale * cotangent.astype(jnp.float32)).astype(jnp.bfloat16)
    up_parts = gather(up_weight)

    def spread(values):
        pieces = []
        for k in range(n_near):
            piece = plain(placer[k * part : (k + 1) * part], values).astype(jnp.bfloat16)
            if steps[k]:
                piece = shift(piece, steps[k], z_total)
            pieces.append(piece)
        return pieces

    def arrive(pieces):
        values = plain(order, jnp.concatenate(pieces, axis=0)).astype(jnp.bfloat16)
        values = exchange(values.reshape(places, n_near * ROWS, width), ("y", "x"))
        return values.reshape(taken, width)

    def leave(values):
        values = values.astype(jnp.bfloat16).reshape(places, n_near * ROWS, width)
        values = exchange(values, ("y", "x"))
        values = rows(order, values.reshape(taken, width)).astype(jnp.bfloat16)
        pieces = []
        for k in range(n_near):
            piece = values[k * part : (k + 1) * part]
            if steps[k]:
                piece = shift(piece, -steps[k], z_total)
            pieces.append(piece)
        return rows(placer, jnp.concatenate(pieces, axis=0))

    here = lax.axis_index("far")

    def far_from(step):
        return (here + step + n_far) % n_far

    tok = spread(tokens)
    cot = spread(scaled)
    down_parts = jnp.zeros((n_far, units, width), jnp.bfloat16)
    down_parts = lax.dynamic_update_index_in_dim(down_parts, down_weight[0], here, 0)
    for step in FAR_STEPS:
        copied = shift(down_weight[0], step * n_near, z_total)
        down_parts = lax.dynamic_update_index_in_dim(down_parts, copied, far_from(-step), 0)
    tok = arrive(tok)
    cot, tok = lax.optimization_barrier((cot, tok))
    cot = arrive(cot)
    cot, up_parts = lax.optimization_barrier((cot, up_parts))

    up = whole(up_parts)
    down_parts, up = lax.optimization_barrier((down_parts, up))
    up = (up, swap_core(up))
    down = whole(down_parts)
    down = (down, swap_core(down))

    preact = [cols(tok, w) for w in up]
    hidden = [smooth(v).astype(jnp.bfloat16) for v in preact]
    down_term = by_owner(*[rows(h, cot) for h in hidden])
    grad_down = summed(down_term)

    hidden_grad = [cols(cot, w) for w in down]
    preact_grad = [
        jax.vjp(smooth, v)[1](g)[0].astype(jnp.bfloat16) for v, g in zip(preact, hidden_grad)
    ]
    up_term = by_owner(*[rows(g, tok) for g in preact_grad])
    grad_up = lax.dynamic_index_in_dim(up_term, here, 0, keepdims=False).astype(jnp.float32)
    for step in FAR_STEPS:
        piece = lax.dynamic_index_in_dim(up_term, far_from(step), 0, keepdims=False)
        piece = shift(piece, step * n_near, z_total)
        grad_up = grad_up + piece.astype(jnp.float32)
    grad_up = grad_up.astype(jnp.bfloat16)[None]

    out = (plain(hidden[0], down[0]) + plain(hidden[1], down[1])).astype(jnp.bfloat16)
    slot_grad = plain(preact_grad[0], up[0]) + plain(preact_grad[1], up[1])
    slot_grad = slot_grad.astype(jnp.bfloat16)
    up_term, out, slot_grad = lax.optimization_barrier((up_term, out, slot_grad))
    output = leave(out)
    token_grad = leave(slot_grad).astype(jnp.bfloat16)
    output_rows = (gate_scale * output).astype(jnp.bfloat16)
    return (output_rows, token_grad, grad_up, grad_down)


def build(finer):
    spread = P(EVERY, None)
    stored = P(EXPERT, ("y", "core"), None)
    specs = (spread, spread, stored, stored)
    return jax.shard_map(
        step,
        mesh=finer,
        in_specs=(spread, spread, spread, spread, stored, stored),
        out_specs=specs,
        check_vma=False,
    )


def solution(mesh):
    return build(Mesh(mesh.devices.reshape(4, 2, 4, 4, 4), EVERY))
```

```python
import jax
import jax.numpy as jnp
from jax import lax
from jax.sharding import Mesh
from jax.sharding import PartitionSpec as P


EVERY = ("y", "core", "far", "near", "x")
EXPERT = ("far", "near", "x")
ROWS = 6
FAR_STEPS = (1, -1, 2)


def smooth(values):
    return jax.nn.gelu(values, approximate=True)


def exchange(values, axes):
    return lax.all_to_all(values, axes, split_axis=0, concat_axis=0, tiled=True)


def cols(left, right):
    return lax.dot_general(
        left, right, (((1,), (1,)), ((), ())), preferred_element_type=jnp.float32
    )


def rows(left, right):
    return lax.dot_general(
        left, right, (((0,), (0,)), ((), ())), preferred_element_type=jnp.float32
    )


def plain(left, right):
    return jnp.dot(left, right, preferred_element_type=jnp.float32)


def swap_core(values):
    return lax.ppermute(values, "core", [(0, 1), (1, 0)])


def shift(values, step, z_total):
    pairs = []
    for core in range(2):
        move = -step if core == 1 and step in (2, -2, z_total // 2) else step
        for z in range(z_total):
            pairs.append((core * z_total + z, core * z_total + (z + move) % z_total))
    return lax.ppermute(values, ("core", "far", "near"), pairs)


def step(tokens, routing, gate_scale, cotangent, up_weight, down_weight):
    count, width = tokens.shape
    units = up_weight.shape[1]
    n_far, n_near, n_x = lax.axis_size("far"), lax.axis_size("near"), lax.axis_size("x")
    z_total = n_far * n_near
    places = n_far * n_x
    part = places * ROWS
    taken = n_near * part
    steps = (0, 1, 2, -1)

    def by_owner(own, other):
        own = (own + swap_core(other.astype(jnp.bfloat16)).astype(jnp.float32))
        own = own.astype(jnp.bfloat16).reshape(n_far, units, width)
        return exchange(own, "y")

    def summed(parts):
        return lax.psum_scatter(parts, "far", scatter_dimension=0, tiled=True)

    ids = routing[:, 0]
    experts = z_total * n_x
    onehot = (ids[:, None] == jnp.arange(experts, dtype=jnp.int32)[None, :]).astype(jnp.float32)
    position = jnp.arange(count, dtype=jnp.int32)
    lower_tri = (position[:, None] >= position[None, :]).astype(jnp.float32)
    counts = plain(lower_tri, onehot)
    slot_rank = (jnp.sum(counts * onehot, axis=1) - 1.0).astype(jnp.int32)
    at_z, at_x = ids // n_x, ids % n_x
    away = (at_z % n_near - lax.axis_index("near") + n_near) % n_near
    slot_index = away * part + ((at_z // n_near) * n_x + at_x) * ROWS + slot_rank
    placer = (jnp.arange(taken, dtype=jnp.int32)[:, None] == slot_index[None, :]).astype(
        jnp.bfloat16
    )
    row = jnp.arange(taken, dtype=jnp.int32)
    source = (row // ROWS) % n_near * part + row // (n_near * ROWS) * ROWS + row % ROWS
    order = (source[:, None] == row[None, :]).astype(jnp.bfloat16)

    scaled = (gate_scale * cotangent.astype(jnp.float32)).astype(jnp.bfloat16)
    stored = jnp.concatenate((up_weight[0], down_weight[0]), axis=1)
    stored = lax.all_gather(stored, "far", axis=0, tiled=False)

    def spread(values):
        pieces = []
        for k in range(n_near):
            piece = plain(placer[k * part : (k + 1) * part], values).astype(jnp.bfloat16)
            if steps[k]:
                piece = shift(piece, steps[k], z_total)
            pieces.append(piece)
        return pieces

    def arrive(pieces):
        values = plain(order, jnp.concatenate(pieces, axis=0)).astype(jnp.bfloat16)
        values = exchange(values.reshape(places, n_near * ROWS, width), ("y", "x"))
        return values.reshape(taken, width)

    def leave(values):
        values = values.astype(jnp.bfloat16).reshape(places, n_near * ROWS, width)
        values = exchange(values, ("y", "x"))
        values = rows(order, values.reshape(taken, width)).astype(jnp.bfloat16)
        pieces = []
        for k in range(n_near):
            piece = values[k * part : (k + 1) * part]
            if steps[k]:
                piece = shift(piece, -steps[k], z_total)
            pieces.append(piece)
        return rows(placer, jnp.concatenate(pieces, axis=0))

    here = lax.axis_index("far")

    def far_from(step):
        return (here + step + n_far) % n_far

    tok = spread(tokens)
    cot = spread(scaled)
    tok = arrive(tok)
    cot, tok = lax.optimization_barrier((cot, tok))
    cot = arrive(cot)
    cot, stored = lax.optimization_barrier((cot, stored))
    stored = exchange(stored, "y")
    stored = stored.reshape(n_far * units, 2 * width)
    stored = (stored, swap_core(stored))
    up = [w[:, :width] for w in stored]
    down = [w[:, width:] for w in stored]

    preact = [cols(tok, w) for w in up]
    hidden = [smooth(v).astype(jnp.bfloat16) for v in preact]
    down_term = by_owner(*[rows(h, cot) for h in hidden])
    grad_down = summed(down_term)

    hidden_grad = [cols(cot, w) for w in down]
    preact_grad = [
        jax.vjp(smooth, v)[1](g)[0].astype(jnp.bfloat16) for v, g in zip(preact, hidden_grad)
    ]
    up_term = by_owner(*[rows(g, tok) for g in preact_grad])
    grad_up = lax.dynamic_index_in_dim(up_term, here, 0, keepdims=False).astype(jnp.float32)
    for step in FAR_STEPS:
        piece = lax.dynamic_index_in_dim(up_term, far_from(step), 0, keepdims=False)
        piece = shift(piece, step * n_near, z_total)
        grad_up = grad_up + piece.astype(jnp.float32)
    grad_up = grad_up.astype(jnp.bfloat16)[None]

    out = (plain(hidden[0], down[0]) + plain(hidden[1], down[1])).astype(jnp.bfloat16)
    slot_grad = plain(preact_grad[0], up[0]) + plain(preact_grad[1], up[1])
    slot_grad = slot_grad.astype(jnp.bfloat16)
    up_term, out, slot_grad = lax.optimization_barrier((up_term, out, slot_grad))
    output = leave(out)
    token_grad = leave(slot_grad).astype(jnp.bfloat16)
    output_rows = (gate_scale * output).astype(jnp.bfloat16)
    return (output_rows, token_grad, grad_up, grad_down)


def build(finer):
    spread = P(EVERY, None)
    stored = P(EXPERT, ("y", "core"), None)
    specs = (spread, spread, stored, stored)
    return jax.shard_map(
        step,
        mesh=finer,
        in_specs=(spread, spread, spread, spread, stored, stored),
        out_specs=specs,
        check_vma=False,
    )


def solution(mesh):
    return build(Mesh(mesh.devices.reshape(4, 2, 4, 4, 4), EVERY))
```

```python
import jax
import jax.numpy as jnp
from jax import lax
from jax.sharding import Mesh
from jax.sharding import PartitionSpec as P


EVERY = ("y", "core", "far", "near", "x")
EXPERT = ("far", "near", "x")
ROWS = 6


def smooth(values):
    return jax.nn.gelu(values, approximate=True)


def exchange(values, axes):
    return lax.all_to_all(values, axes, split_axis=0, concat_axis=0, tiled=True)


def cols(left, right):
    return lax.dot_general(
        left, right, (((1,), (1,)), ((), ())), preferred_element_type=jnp.float32
    )


def rows(left, right):
    return lax.dot_general(
        left, right, (((0,), (0,)), ((), ())), preferred_element_type=jnp.float32
    )


def plain(left, right):
    return jnp.dot(left, right, preferred_element_type=jnp.float32)


def swap_core(values):
    return lax.ppermute(values, "core", [(0, 1), (1, 0)])


def shift(values, step, z_total):
    pairs = []
    for core in range(2):
        move = -step if core == 1 and step in (2, -2, z_total // 2) else step
        for z in range(z_total):
            pairs.append((core * z_total + z, core * z_total + (z + move) % z_total))
    return lax.ppermute(values, ("core", "far", "near"), pairs)


def step(tokens, routing, gate_scale, cotangent, up_weight, down_weight):
    count, width = tokens.shape
    units = up_weight.shape[1]
    n_far, n_near, n_x = lax.axis_size("far"), lax.axis_size("near"), lax.axis_size("x")
    z_total = n_far * n_near
    places = n_far * n_x
    part = places * ROWS
    taken = n_near * part
    steps = (0, 1, 2, -1)

    ids = routing[:, 0]
    experts = z_total * n_x
    onehot = (ids[:, None] == jnp.arange(experts, dtype=jnp.int32)[None, :]).astype(jnp.float32)
    position = jnp.arange(count, dtype=jnp.int32)
    lower_tri = (position[:, None] >= position[None, :]).astype(jnp.float32)
    counts = plain(lower_tri, onehot)
    slot_rank = (jnp.sum(counts * onehot, axis=1) - 1.0).astype(jnp.int32)
    at_z, at_x = ids // n_x, ids % n_x
    away = (at_z % n_near - lax.axis_index("near") + n_near) % n_near
    slot_index = away * part + ((at_z // n_near) * n_x + at_x) * ROWS + slot_rank
    placer = (jnp.arange(taken, dtype=jnp.int32)[:, None] == slot_index[None, :]).astype(
        jnp.bfloat16
    )
    row = jnp.arange(taken, dtype=jnp.int32)
    source = (row // ROWS) % n_near * part + row // (n_near * ROWS) * ROWS + row % ROWS
    order = (source[:, None] == row[None, :]).astype(jnp.bfloat16)

    scaled = (gate_scale * cotangent.astype(jnp.float32)).astype(jnp.bfloat16)
    stored = jnp.concatenate((up_weight[0], down_weight[0]), axis=1)
    stored = lax.all_gather(stored, "far", axis=0, tiled=False)

    def spread(values):
        pieces = []
        for k in range(n_near):
            piece = plain(placer[k * part : (k + 1) * part], values).astype(jnp.bfloat16)
            if steps[k]:
                piece = shift(piece, steps[k], z_total)
            pieces.append(piece)
        return pieces

    def arrive(pieces):
        values = plain(order, jnp.concatenate(pieces, axis=0)).astype(jnp.bfloat16)
        values = exchange(values.reshape(places, n_near * ROWS, width), ("y", "x"))
        return values.reshape(taken, width)

    def leave(values):
        values = values.astype(jnp.bfloat16).reshape(places, n_near * ROWS, width)
        values = exchange(values, ("y", "x"))
        values = rows(order, values.reshape(taken, width)).astype(jnp.bfloat16)
        pieces = []
        for k in range(n_near):
            piece = values[k * part : (k + 1) * part]
            if steps[k]:
                piece = shift(piece, -steps[k], z_total)
            pieces.append(piece)
        return rows(placer, jnp.concatenate(pieces, axis=0))

    tok = spread(tokens)
    cot = spread(scaled)
    tok = arrive(tok)
    cot, tok = lax.optimization_barrier((cot, tok))
    cot = arrive(cot)
    cot, stored = lax.optimization_barrier((cot, stored))
    stored = exchange(stored, "y")
    stored = stored.reshape(n_far * units, 2 * width)
    stored = (stored, swap_core(stored))
    up = [w[:, :width] for w in stored]
    down = [w[:, width:] for w in stored]

    preact = [cols(tok, w) for w in up]
    hidden = [smooth(v).astype(jnp.bfloat16) for v in preact]
    hidden_grad = [cols(cot, w) for w in down]
    preact_grad = [
        jax.vjp(smooth, v)[1](g)[0].astype(jnp.bfloat16) for v, g in zip(preact, hidden_grad)
    ]
    term = [
        jnp.concatenate((rows(g, tok), rows(h, cot)), axis=1)
        for g, h in zip(preact_grad, hidden)
    ]
    term = term[0] + swap_core(term[1].astype(jnp.bfloat16)).astype(jnp.float32)
    term = term.astype(jnp.bfloat16).reshape(n_far, units, 2 * width)
    term = exchange(term, "y")
    total = lax.psum_scatter(term, "far", scatter_dimension=0, tiled=True)
    grad_up, grad_down = total[:, :, :width], total[:, :, width:]

    out = (plain(hidden[0], down[0]) + plain(hidden[1], down[1])).astype(jnp.bfloat16)
    slot_grad = plain(preact_grad[0], up[0]) + plain(preact_grad[1], up[1])
    slot_grad = slot_grad.astype(jnp.bfloat16)
    term, out, slot_grad = lax.optimization_barrier((term, out, slot_grad))
    output = leave(out)
    token_grad = leave(slot_grad).astype(jnp.bfloat16)
    output_rows = (gate_scale * output).astype(jnp.bfloat16)
    return (output_rows, token_grad, grad_up, grad_down)


def build(finer):
    spread = P(EVERY, None)
    stored = P(EXPERT, ("y", "core"), None)
    specs = (spread, spread, stored, stored)
    return jax.shard_map(
        step,
        mesh=finer,
        in_specs=(spread, spread, spread, spread, stored, stored),
        out_specs=specs,
        check_vma=False,
    )


def solution(mesh):
    return build(Mesh(mesh.devices.reshape(4, 2, 4, 4, 4), EVERY))
```

```python
import jax
import jax.numpy as jnp
from jax import lax
from jax.sharding import Mesh
from jax.sharding import PartitionSpec as P


EVERY = ("y", "core", "far", "near", "x")
EXPERT = ("far", "near", "x")
ROWS = 6


def smooth(values):
    return jax.nn.gelu(values, approximate=True)


def exchange(values, axes):
    return lax.all_to_all(values, axes, split_axis=0, concat_axis=0, tiled=True)


def cols(left, right):
    return lax.dot_general(
        left, right, (((1,), (1,)), ((), ())), preferred_element_type=jnp.float32
    )


def rows(left, right):
    return lax.dot_general(
        left, right, (((0,), (0,)), ((), ())), preferred_element_type=jnp.float32
    )


def plain(left, right):
    return jnp.dot(left, right, preferred_element_type=jnp.float32)


def swap_core(values):
    return lax.ppermute(values, "core", [(0, 1), (1, 0)])


def shift(values, step, z_total):
    pairs = []
    for core in range(2):
        move = -step if core == 1 and step in (2, -2, z_total // 2) else step
        for z in range(z_total):
            pairs.append((core * z_total + z, core * z_total + (z + move) % z_total))
    return lax.ppermute(values, ("core", "far", "near"), pairs)


def step(tokens, routing, gate_scale, cotangent, up_weight, down_weight):
    count, width = tokens.shape
    units = up_weight.shape[1]
    n_far, n_near, n_x = lax.axis_size("far"), lax.axis_size("near"), lax.axis_size("x")
    z_total = n_far * n_near
    places = n_far * n_x
    part = places * ROWS
    taken = n_near * part
    steps = (0, 1, 2, -1)

    ids = routing[:, 0]
    experts = z_total * n_x
    onehot = (ids[:, None] == jnp.arange(experts, dtype=jnp.int32)[None, :]).astype(jnp.float32)
    position = jnp.arange(count, dtype=jnp.int32)
    lower_tri = (position[:, None] >= position[None, :]).astype(jnp.float32)
    counts = plain(lower_tri, onehot)
    slot_rank = (jnp.sum(counts * onehot, axis=1) - 1.0).astype(jnp.int32)
    at_z, at_x = ids // n_x, ids % n_x
    away = (at_z % n_near - lax.axis_index("near") + n_near) % n_near
    slot_index = away * part + ((at_z // n_near) * n_x + at_x) * ROWS + slot_rank
    placer = (jnp.arange(taken, dtype=jnp.int32)[:, None] == slot_index[None, :]).astype(
        jnp.bfloat16
    )
    row = jnp.arange(taken, dtype=jnp.int32)
    source = (row // ROWS) % n_near * part + row // (n_near * ROWS) * ROWS + row % ROWS
    order = (source[:, None] == row[None, :]).astype(jnp.bfloat16)

    scaled = (gate_scale * cotangent.astype(jnp.float32)).astype(jnp.bfloat16)
    stored = jnp.concatenate((up_weight[0], down_weight[0]), axis=1)
    stored = lax.all_gather(stored, "far", axis=0, tiled=False)

    def spread(values):
        pieces = []
        for k in range(n_near):
            piece = plain(placer[k * part : (k + 1) * part], values).astype(jnp.bfloat16)
            if steps[k]:
                piece = shift(piece, steps[k], z_total)
            pieces.append(piece)
        return pieces

    def arrive(pieces):
        values = plain(order, jnp.concatenate(pieces, axis=0)).astype(jnp.bfloat16)
        values = exchange(values.reshape(places, n_near * ROWS, -1), ("y", "x"))
        return values.reshape(taken, -1)

    def leave(values):
        values = values.astype(jnp.bfloat16).reshape(places, n_near * ROWS, width)
        values = exchange(values, ("y", "x"))
        values = rows(order, values.reshape(taken, width)).astype(jnp.bfloat16)
        pieces = []
        for k in range(n_near):
            piece = values[k * part : (k + 1) * part]
            if steps[k]:
                piece = shift(piece, -steps[k], z_total)
            pieces.append(piece)
        return rows(placer, jnp.concatenate(pieces, axis=0))

    arrived = arrive(spread(jnp.concatenate((tokens, scaled), axis=1)))
    arrived, stored = lax.optimization_barrier((arrived, stored))
    tok, cot = arrived[:, :width], arrived[:, width:]
    stored = exchange(stored, "y")
    stored = stored.reshape(n_far * units, 2 * width)
    stored = (stored, swap_core(stored))
    up = [w[:, :width] for w in stored]
    down = [w[:, width:] for w in stored]

    preact = [cols(tok, w) for w in up]
    hidden = [smooth(v).astype(jnp.bfloat16) for v in preact]
    hidden_grad = [cols(cot, w) for w in down]
    preact_grad = [
        jax.vjp(smooth, v)[1](g)[0].astype(jnp.bfloat16) for v, g in zip(preact, hidden_grad)
    ]
    term = [
        jnp.concatenate((rows(g, tok), rows(h, cot)), axis=1)
        for g, h in zip(preact_grad, hidden)
    ]
    term = term[0] + swap_core(term[1].astype(jnp.bfloat16)).astype(jnp.float32)
    term = term.astype(jnp.bfloat16).reshape(n_far, units, 2 * width)
    term = exchange(term, "y")
    total = lax.psum_scatter(term, "far", scatter_dimension=0, tiled=True)
    grad_up, grad_down = total[:, :, :width], total[:, :, width:]

    out = (plain(hidden[0], down[0]) + plain(hidden[1], down[1])).astype(jnp.bfloat16)
    slot_grad = plain(preact_grad[0], up[0]) + plain(preact_grad[1], up[1])
    slot_grad = slot_grad.astype(jnp.bfloat16)
    term, out, slot_grad = lax.optimization_barrier((term, out, slot_grad))
    output = leave(out)
    token_grad = leave(slot_grad).astype(jnp.bfloat16)
    output_rows = (gate_scale * output).astype(jnp.bfloat16)
    return (output_rows, token_grad, grad_up, grad_down)


def build(finer):
    spread = P(EVERY, None)
    stored = P(EXPERT, ("y", "core"), None)
    specs = (spread, spread, stored, stored)
    return jax.shard_map(
        step,
        mesh=finer,
        in_specs=(spread, spread, spread, spread, stored, stored),
        out_specs=specs,
        check_vma=False,
    )


def solution(mesh):
    return build(Mesh(mesh.devices.reshape(4, 2, 4, 4, 4), EVERY))
```
